512 devices in a mesh: row: 8 (over x, z_hi), col: 64 (over y, z_lo, core).
Axes of the slice: x: 4, y: 8, z: 8 (z_hi: 2, z_lo: 4; z = z_hi * 4 + z_lo), core: 2. Of those that a mesh axis runs over, the one named last changes fastest.
Arguments:
- sigma_anc: bfloat16 [4096, 4096], P('row', 'col'), as said below
- top_panel: bfloat16 [4096, 4096], P('row', 'col'), may hold values from -0.09375 to 0.09375
- top_dinv: bfloat16 [4096, 4096], P('row', 'col'), as said below
- low_upper: bfloat16 [4096, 4096], P('row', 'col'), may hold values from -0.09375 to 0.09375
- low_ancestor: bfloat16 [4096, 4096], P('row', 'col'), may hold values from -0.09375 to 0.09375
- low_dinv: bfloat16 [4096, 4096], P('row', 'col'), as said below
- low_rows: int32 [16], replicated, may hold values from 0 to 31, as said below
Outputs:
- top_off: bfloat16 [4096, 4096], P('row', 'col')
- top_diag: bfloat16 [4096, 4096], P('row', 'col')
- low_top: bfloat16 [4096, 4096], P('row', 'col')
- low_anc: bfloat16 [4096, 4096], P('row', 'col')
- low_diag: bfloat16 [4096, 4096], P('row', 'col')
The draws below stay inside these ranges and needn't reach their ends.
Inputs may be any that keep to these rules, and one draw needn't show every extreme that they name: `low_rows`: 16 distinct block indices; the first and the last ancestor block are always among them. `sigma_anc`: symmetric. `top_dinv`: symmetric. `low_dinv`: symmetric.
All inputs are finite; a program needn't handle non-finite values.
Results may differ from the reference program's by a relative error of at most 0.0085.
Values may be sent and summed in bfloat16 or wider, within the bound.
A program may use at most 64 MiB of HBM per device.

```python
import jax
import jax.numpy as jnp

BLOCK = 128
W = 4096
SA = 4096
LOW_BLOCKS = 16
NBLK = 32


def symmetric_block(key, salt, order, spread, low_diag, high_diag):
    seeded = jax.random.fold_in(key, salt)
    first, second = jax.random.split(seeded, 2)
    normal_part = jax.random.normal(first, (order, order), jnp.float32)
    diagonal = jax.random.uniform(second, (order,), jnp.float32, low_diag, high_diag)
    identity = (jnp.arange(order)[:, None] == jnp.arange(order)[None, :]).astype(jnp.float32)
    matrix = (normal_part + normal_part.T) * (0.7071 * spread) + identity * diagonal[None, :]
    return matrix


def draw_sigma_anc(key, part):
    return symmetric_block(key, 10, SA, 1.0, 1.0, 3.0).astype(jnp.bfloat16)


def draw_top_dinv(key, part):
    return symmetric_block(key, 11, W, 0.3, 1.0, 3.0).astype(jnp.bfloat16)


def draw_low_dinv(key, part):
    return symmetric_block(key, 12, W, 0.3, 1.0, 3.0).astype(jnp.bfloat16)


def draw_low_rows(key, part):
    seeded = jax.random.fold_in(key, 13)
    inner = jax.random.permutation(seeded, NBLK - 2)[:LOW_BLOCKS - 2].astype(jnp.int32) + 1
    first_block = jnp.zeros((1,), jnp.int32)
    last_block = jnp.full((1,), NBLK - 1, jnp.int32)
    return jnp.concatenate([first_block, inner, last_block])


def block_scale(key, extent, pieces, smallest, high):
    loudness = 1.0
    for dim, shards_of in pieces:
        steps = jax.random.uniform(jax.random.fold_in(jax.random.fold_in(key, 6), dim), (shards_of,), jnp.float32, smallest / len(pieces), high / len(pieces))
        loudness = loudness * jnp.repeat(jnp.exp(steps), extent[dim] // shards_of).reshape((-1,) + (1,) * (len(extent) - 1 - dim))
    return loudness


def gaussian(stream_key, shape, deviation, bound, cuts=(), held_as=jnp.bfloat16):
    drawn = deviation * jax.random.normal(stream_key, shape, jnp.float32)
    if cuts:
        drawn = drawn * block_scale(stream_key, shape, cuts, -0.22, 0.18)
    return jnp.clip(drawn, -bound, bound).astype(held_as)


def setup_inputs(seed: int = 0) -> dict:
    arg_keys = jax.random.split(jax.random.key(seed), 8)
    sigma_anc = draw_sigma_anc(jax.random.fold_in(arg_keys[7], 71), 0)
    top_panel = gaussian(arg_keys[1], (SA, W), SA ** -0.5, 0.09375, ((0, 8), (1, 64)))
    top_dinv = draw_top_dinv(jax.random.fold_in(arg_keys[7], 71), 0)
    low_upper = gaussian(arg_keys[3], (W, W), W ** -0.5, 0.09375, ((0, 8), (1, 64)))
    low_ancestor = gaussian(arg_keys[4], (SA, W), SA ** -0.5, 0.09375, ((0, 8), (1, 64)))
    low_dinv = draw_low_dinv(jax.random.fold_in(arg_keys[7], 71), 0)
    low_rows = draw_low_rows(jax.random.fold_in(arg_keys[7], 71), 0)
    return dict(sigma_anc=sigma_anc, top_panel=top_panel, top_dinv=top_dinv, low_upper=low_upper, low_ancestor=low_ancestor, low_dinv=low_dinv, low_rows=low_rows)


def reference(sigma_anc, top_panel, top_dinv, low_upper, low_ancestor, low_dinv, low_rows):
    row_ids = jnp.arange(SA, dtype=jnp.int32) // BLOCK
    in_pattern = jnp.any(row_ids[:, None] == low_rows[None, :], axis=1).astype(jnp.float32)[:, None]
    masked = (low_ancestor.astype(jnp.float32) * in_pattern).astype(jnp.bfloat16)
    top_off = (-jnp.dot(sigma_anc, top_panel, preferred_element_type=jnp.float32)).astype(jnp.bfloat16)
    top_diag = (top_dinv.astype(jnp.float32) - jnp.dot(top_off.T, top_panel, preferred_element_type=jnp.float32)).astype(jnp.bfloat16)
    cross = jnp.dot(top_off.T, masked, preferred_element_type=jnp.float32)
    ancestor_sum = jnp.dot(top_off, low_upper, preferred_element_type=jnp.float32) + jnp.dot(sigma_anc, masked, preferred_element_type=jnp.float32)
    low_anc = (-in_pattern * ancestor_sum).astype(jnp.bfloat16)
    low_top = (-(jnp.dot(top_diag, low_upper, preferred_element_type=jnp.float32) + cross)).astype(jnp.bfloat16)
    low_terms = jnp.dot(low_top.T, low_upper, preferred_element_type=jnp.float32) + jnp.dot(low_anc.T, masked, preferred_element_type=jnp.float32)
    low_diag = (low_dinv.astype(jnp.float32) - low_terms).astype(jnp.bfloat16)
    return (top_off, top_diag, low_top, low_anc, low_diag)
```

```python
import jax
import jax.numpy as jnp
from jax import lax
from jax.experimental import pallas as pl
from jax.experimental.pallas import tpu as pltpu
from jax.sharding import PartitionSpec as P

BLOCK = 128
NX, NH, NY, NL, NC = 4, 2, 8, 4, 2
F32, BF16 = jnp.float32, jnp.bfloat16
T, S, TD, U, M = range(5)


def dot_nn(left, right):
    return jnp.dot(left, right, preferred_element_type=F32)


def dot_nt(left, right):
    return lax.dot_general(left, right, (((1,), (1,)), ((), ())), preferred_element_type=F32)


def kernel(
    pat_ref, t_ref, s_ref, td_ref, u_ref, m_ref, ld_ref,
    o_out, d_out, lt_out, la_out, ldiag_out,
    panel, cols, xb, gb, part, part16, got, half, send_half, got_half,
    local_sem, zs, zr, ys, yr, cs, cr, ms, mr, ms2, mr2, mc_s, mc_r, ah_s, ah_r, ax_s, ax_r, rx_s, rx_r, rh_s, rh_r,
):
    row, col = lax.axis_index("row"), lax.axis_index("col")
    x, h = row // NH, row % NH
    y, l, c = col // (NL * NC), (col // NC) % NL, col % NC

    def dev(x=x, h=h, y=y, l=l, c=c):
        return (x * NH + h, (y * NL + l) * NC + c)

    def wrap(v, n):
        return lax.rem(v + n, n)

    barrier = pltpu.get_barrier_semaphore()
    peers = (
        [dev(l=wrap(l + d, NL)) for d in range(1, NL)]
        + [dev(y=wrap(y + 1, NY)), dev(y=wrap(y - 1, NY)), dev(c=1 - c), dev(h=1 - h)]
        + [dev(x=wrap(x + d, NX)) for d in range(1, NX)]
    )
    for peer in peers:
        pl.semaphore_signal(barrier, inc=1, device_id=peer, device_id_type=pl.DeviceIdType.MESH)
    pl.semaphore_wait(barrier, len(peers))

    sent = []

    def put(src, dst, send, recv, peer):
        copy = pltpu.make_async_remote_copy(
            src_ref=src, dst_ref=dst, send_sem=send, recv_sem=recv,
            device_id=peer, device_id_type=pl.DeviceIdType.MESH,
        )
        copy.start()
        sent.append(copy)
        return copy

    inputs = {T: t_ref, S: s_ref, TD: td_ref, U: u_ref, M: m_ref}
    own = {}
    for p in range(5):
        own[p] = pltpu.make_async_copy(inputs[p], panel.at[p, y, l, c], local_sem.at[p])
        own[p].start()

    def z_send(p):
        return [
            put(inputs[p], panel.at[p, y, l, c], zs.at[p, d - 1], zr.at[p, d - 1], dev(l=wrap(l + d, NL)))
            for d in range(1, NL)
        ]

    z_copies, y_copies, c_copies = {}, {}, {}

    def slab(p, where, part):
        if part is None:
            return panel.at[p, where, :, c]
        return panel.at[p, where, pl.ds(part * (NL // 2), NL // 2), c]

    def to_core(p, where, part, k):
        ref = slab(p, where, part)
        c_copies.setdefault(p, []).append(put(ref, ref, cs.at[p, k], cr.at[p, k], dev(c=1 - c)))

    def ring(p, step):
        up, down = dev(y=wrap(y + 1, NY)), dev(y=wrap(y - 1, NY))
        if step == 0:
            own[p].wait()
            for copy in z_copies[p]:
                copy.wait_recv()
            mine = slab(p, y, None)
            y_copies[p] = [
                put(mine, mine, ys.at[p, 0, 0], yr.at[p, 0, 0], up),
                put(mine, mine, ys.at[p, 1, 0], yr.at[p, 1, 0], down),
            ]
            to_core(p, y, None, 0)
            return
        before = y_copies[p]
        before[0].wait_recv()
        before[1].wait_recv()
        below, above = wrap(y - step, NY), wrap(y + step, NY)
        if step < NY // 2:
            last = step == NY // 2 - 1
            low, high = slab(p, below, 0 if last else None), slab(p, above, 1 if last else None)
            y_copies[p] = [
                put(low, low, ys.at[p, 0, step], yr.at[p, 0, step], up),
                put(high, high, ys.at[p, 1, step], yr.at[p, 1, step], down),
            ]
            to_core(p, below, None, 2 * step - 1)
            to_core(p, above, None, 2 * step)
        else:
            to_core(p, below, 0, 2 * step - 1)
            to_core(p, above, 1, 2 * step)

    def full(p):
        for copy in c_copies[p]:
            copy.wait_recv()

    rows = m_ref.shape[0]
    m_last = {}

    def m_piece(where, part):
        if part is None:
            return panel.at[M, where, l, c]
        return panel.at[M, where, l, c, pl.ds(part * (rows // 2), rows // 2)]

    def m_ring(step):
        up, down = dev(y=wrap(y + 1, NY)), dev(y=wrap(y - 1, NY))
        if step == 0:
            mine = m_piece(y, None)
            m_last["y"] = [
                put(m_ref, mine, ms.at[0, 0], mr.at[0, 0], up),
                put(m_ref, mine, ms.at[1, 0], mr.at[1, 0], down),
            ]
            return
        for copy in m_last["y"]:
            copy.wait_recv()
        below, above = wrap(y - step, NY), wrap(y + step, NY)
        if step < NY // 2:
            last = step == NY // 2 - 1
            low, high = m_piece(below, 0 if last else None), m_piece(above, 1 if last else None)
            m_last["y"] = [
                put(low, low, ms.at[0, step], mr.at[0, step], up),
                put(high, high, ms.at[1, step], mr.at[1, step], down),
            ]
        else:
            own[M].wait()
            column = panel.at[M, :, l, c]
            m_last["z"] = [
                put(column, column, ms2.at[d - 1], mr2.at[d - 1], dev(l=wrap(l + d, NL))) for d in range(1, NL)
            ]

    def m_core():
        for copy in m_last["z"]:
            copy.wait_recv()
        mine = panel.at[M, :, :, c]
        m_last["c"] = put(mine, mine, mc_s.at[0], mc_r.at[0], dev(c=1 - c))

    ag, ag_local = {}, {}

    def ag_start(i, src):
        mine = cols.at[i, row]
        ag_local[i] = pltpu.make_async_copy(src, mine, local_sem.at[5 + i])
        ag_local[i].start()
        ag[i] = [put(src, mine, ah_s.at[i], ah_r.at[i], dev(h=1 - h))]
        for d in range(1, NX):
            ag[i].append(put(src, mine, ax_s.at[i, 0, d - 1], ax_r.at[i, 0, d - 1], dev(x=wrap(x + d, NX))))

    def ag_forward(i):
        ag[i][0].wait_recv()
        other = cols.at[i, x * NH + 1 - h]
        for d in range(1, NX):
            ag[i].append(put(other, other, ax_s.at[i, 1, d - 1], ax_r.at[i, 1, d - 1], dev(x=wrap(x + d, NX))))

    def ag_wait(i):
        ag_local[i].wait()
        for copy in ag[i][1:]:
            copy.wait_recv()

    def times(i, p):
        def one(k, total):
            return total + dot_nn(cols[i, k], panel[p, k].reshape(512, 512))

        return lax.fori_loop(0, NY, one, jnp.zeros((64, 512), F32))

    rs = {}

    def rs_start(j, terms):
        @pl.loop(0, NY)
        def _(k):
            total = None
            for left, p, sign in terms:
                value = dot_nt(left, panel[p, k].reshape(512, 512))
                value = -value if sign < 0 else value
                total = value if total is None else total + value
            part[k] = total
            part16[j, k] = total.astype(BF16)

        rs[j] = []
        for d in range(1, NX):
            to = wrap(x + d, NX)
            rs[j].append(
                put(part16.at[j, pl.ds(to * NH, NH)], got.at[j, d - 1], rx_s.at[j, d - 1], rx_r.at[j, d - 1], dev(x=to))
            )
        half[j] = part[pl.ds(x * NH, NH)]

    def rs_middle(j):
        for copy in rs[j]:
            copy.wait_recv()
        send_half[j] = (
            half[j, 1 - h] + got[j, 0, 1 - h].astype(F32) + got[j, 1, 1 - h].astype(F32) + got[j, 2, 1 - h].astype(F32)
        ).astype(BF16)
        rs[j] = put(send_half.at[j], got_half.at[j], rh_s.at[j], rh_r.at[j], dev(h=1 - h))

    def rs_end(j):
        total = half[j, h] + got[j, 0, h].astype(F32) + got[j, 1, h].astype(F32) + got[j, 2, h].astype(F32)
        rs[j].wait_recv()
        return total + got_half[j].astype(F32)

    RT, RU, RX = 0, 1, 2
    z_copies[T] = z_send(T)
    m_ring(0)
    ag_start(RU, u_ref)
    z_copies[S] = z_send(S)
    ag_start(RT, t_ref)
    m_ring(1)
    z_copies[TD] = z_send(TD)
    z_copies[U] = z_send(U)
    m_ring(2)
    ring(T, 0)
    m_ring(3)
    ring(S, 0)
    m_ring(4)
    ag_forward(RU)
    ring(T, 1)
    ag_forward(RT)
    ring(S, 1)
    ring(T, 2)
    ring(S, 2)
    ring(T, 3)
    ring(TD, 0)
    ring(S, 3)
    ring(T, 4)
    ring(U, 0)
    ag_wait(RU)
    full(T)
    xb[...] = (m_ref[...].astype(F32) - times(RU, T)).astype(BF16)
    ag_start(RX, xb)
    ring(S, 4)
    ring(TD, 1)
    ring(U, 1)
    ag_wait(RT)
    full(S)
    o_out[...] = (-times(RT, S)).astype(BF16)
    ag_forward(RX)
    ring(TD, 2)
    ring(U, 2)
    rs_start(0, [(o_out[...], T, 1)])
    ag_wait(RX)
    g = times(RX, S)
    gb[...] = g.astype(BF16)
    la_out[...] = (-(pat_ref[...] * g)).astype(BF16)
    rs_start(1, [(gb[...], T, 1)])
    ring(TD, 3)
    ring(U, 3)
    rs_middle(0)
    rs_middle(1)
    ring(TD, 4)
    ring(U, 4)
    full(TD)
    e = times(RU, TD)
    lt_out[...] = (rs_end(1) - e).astype(BF16)
    m_core()
    d_out[...] = (td_ref[...].astype(F32) - rs_end(0)).astype(BF16)
    full(U)
    m_last["c"].wait_recv()
    rs_start(2, [(lt_out[...], U, 1), (gb[...], M, -1)])
    rs_middle(2)
    ldiag_out[...] = (ld_ref[...].astype(F32) - rs_end(2)).astype(BF16)
    for copy in sent:
        copy.wait_send()


def body(sigma_anc, top_panel, top_dinv, low_upper, low_ancestor, low_dinv, low_rows):
    rows_here, width = sigma_anc.shape
    row_ids = (lax.axis_index("row") * rows_here + jnp.arange(rows_here, dtype=jnp.int32)) // BLOCK
    in_pattern = jnp.any(row_ids[None, :] == low_rows[:, None], axis=0).astype(F32)[None, :]
    masked = (low_ancestor.T.astype(F32) * in_pattern).astype(BF16)
    block = (width, rows_here)
    dma, vmem = pltpu.SemaphoreType.DMA, pltpu.VMEM
    outs = pl.pallas_call(
        kernel,
        out_shape=[jax.ShapeDtypeStruct(block, BF16)] * 5,
        in_specs=[pl.BlockSpec(memory_space=pltpu.VMEM)] * 7,
        out_specs=[pl.BlockSpec(memory_space=pltpu.VMEM)] * 5,
        scratch_shapes=[
            vmem((5, NY, NL, NC) + block, BF16),
            vmem((3, NX * NH) + block, BF16),
            vmem(block, BF16),
            vmem(block, BF16),
            vmem((NY,) + block, F32),
            vmem((3, NY) + block, BF16),
            vmem((3, NX - 1, NH) + block, BF16),
            vmem((3, NH) + block, F32),
            vmem((3,) + block, BF16),
            vmem((3,) + block, BF16),
            dma((8,)),
            dma((4, 3)), dma((4, 3)),
            dma((4, 2, 4)), dma((4, 2, 4)),
            dma((4, 9)), dma((4, 9)),
            dma((2, 4)), dma((2, 4)),
            dma((3,)), dma((3,)),
            dma((1,)), dma((1,)),
            dma((3,)), dma((3,)),
            dma((3, 2, 3)), dma((3, 2, 3)),
            dma((3, 3)), dma((3, 3)),
            dma((3,)), dma((3,)),
        ],
        compiler_params=pltpu.CompilerParams(
            collective_id=0, has_side_effects=True, vmem_limit_bytes=56 * 1024 * 1024
        ),
    )(in_pattern, top_panel.T, sigma_anc.T, top_dinv.T, low_upper.T, masked, low_dinv.T)
    return tuple(out.T for out in outs)


def solution(mesh):
    return jax.shard_map(
        body,
        mesh=mesh,
        in_specs=(P("row", "col"),) * 6 + (P(),),
        out_specs=(P("row", "col"),) * 5,
        check_vma=False,
    )
```

```python
import jax
import jax.numpy as jnp
from jax import lax
from jax.experimental import pallas as pl
from jax.experimental.pallas import tpu as pltpu
from jax.sharding import PartitionSpec as P

BLOCK = 128
NX, NH, NY, NL, NC = 4, 2, 8, 4, 2
F32, BF16 = jnp.float32, jnp.bfloat16
T, S, U = range(3)
TD, M = range(2)
ROWS, COLS = 64, 512
SUB = COLS // NL


def dot_nn(left, right):
    return jnp.dot(left, right, preferred_element_type=F32)


def dot_nt(left, right):
    return lax.dot_general(left, right, (((1,), (1,)), ((), ())), preferred_element_type=F32)


def kernel(
    low_rows, t_ref, s_ref, td_ref, u_ref, a_ref, ld_ref,
    o_out, d_out, lt_out, la_out, ldiag_out,
    panel, thin, cols, cols3, mb, xb, gb, gz, ez, ez16, got_e,
    part, part16, got, send_half, got_half,
    part3, part3_16, got3, send_half3, got_half3, quarter, joined,
    local_sem, zs, zr, ys, yr, cs, cr, ts, tr, tcs, tcr, us, ur,
    ah_s, ah_r, ax_s, ax_r, es, er, gs, gr, rx_s, rx_r, rh_s, rh_r, qs, qr,
):
    row, col = lax.axis_index("row"), lax.axis_index("col")
    x, h = row // NH, row % NH
    y, l, c = col // (NL * NC), (col // NC) % NL, col % NC

    def dev(x=x, h=h, y=y, l=l, c=c):
        return (x * NH + h, (y * NL + l) * NC + c)

    def wrap(v, n):
        return lax.rem(v + n, n)

    up, down = dev(y=wrap(y + 1, NY)), dev(y=wrap(y - 1, NY))
    l_peers = [dev(l=wrap(l + d, NL)) for d in range(1, NL)]
    x_peers = [dev(x=wrap(x + d, NX)) for d in range(1, NX)]

    barrier = pltpu.get_barrier_semaphore()
    peers = l_peers + [up, down, dev(c=1 - c), dev(h=1 - h)] + x_peers
    for peer in peers:
        pl.semaphore_signal(barrier, inc=1, device_id=peer, device_id_type=pl.DeviceIdType.MESH)

    blocks = row * (COLS // BLOCK) + lax.broadcasted_iota(jnp.int32, (1, COLS), 1) // BLOCK
    pattern = jnp.zeros((1, COLS), F32)
    for j in range(low_rows.shape[0]):
        pattern = jnp.where(blocks == low_rows[j], 1.0, pattern)
    mb[...] = (a_ref[...].astype(F32) * pattern).astype(BF16)

    pl.semaphore_wait(barrier, len(peers))

    sent = []

    def put(src, dst, send, recv, peer):
        copy = pltpu.make_async_remote_copy(
            src_ref=src, dst_ref=dst, send_sem=send, recv_sem=recv,
            device_id=peer, device_id_type=pl.DeviceIdType.MESH,
        )
        copy.start()
        sent.append(copy)
        return copy

    def arrived(copies):
        for copy in copies:
            copy.wait_recv()

    local = []

    def move(src, dst):
        copy = pltpu.make_async_copy(src, dst, local_sem.at[len(local)])
        copy.start()
        local.append(copy)
        return copy

    inputs = {T: t_ref, S: s_ref, U: u_ref}
    own, z_copies, y_copies, c_copies = {}, {}, {}, {}

    def z_send(p):
        own[p] = move(inputs[p], panel.at[p, y, l, c])
        z_copies[p] = [
            put(inputs[p], panel.at[p, y, l, c], zs.at[p, d], zr.at[p, d], l_peers[d]) for d in range(NL - 1)
        ]

    def slab(p, where, part):
        if part is None:
            return panel.at[p, where, :, c]
        return panel.at[p, where, pl.ds(part * (NL // 2), NL // 2), c]

    def to_core(p, where, part):
        ref = slab(p, where, part)
        k = len(c_copies.setdefault(p, []))
        c_copies[p].append(put(ref, ref, cs.at[p, k], cr.at[p, k], dev(c=1 - c)))

    def both(p, n, low, high):
        y_copies.setdefault(p, []).append([
            put(low, low, ys.at[p, 0, n], yr.at[p, 0, n], up),
            put(high, high, ys.at[p, 1, n], yr.at[p, 1, n], down),
        ])

    def ring(p, n):
        if n == 0:
            own[p].wait()
            arrived(z_copies[p])
            both(p, 0, slab(p, y, 0), slab(p, y, 1))
            both(p, 1, slab(p, y, 1), slab(p, y, 0))
            to_core(p, y, None)
            return
        arrived(y_copies[p][n - 1])
        step, second = (n + 1) // 2, (n + 1) % 2
        below, above = wrap(y - step, NY), wrap(y + step, NY)
        if n <= 5:
            both(p, n + 1, slab(p, below, second), slab(p, above, 1 - second))
        if n == 7:
            to_core(p, below, 0)
            to_core(p, above, 1)
        elif second:
            to_core(p, below, None)
            to_core(p, above, None)

    def full(p):
        arrived(c_copies[p])

    thin_inputs = {TD: td_ref, M: mb}
    thin_own, thin_last, thin_core = {}, {}, {}

    def piece(q, where, part):
        if part is None:
            return thin.at[q, where, c]
        return thin.at[q, where, c, pl.ds(part * (ROWS // 2), ROWS // 2)]

    def thin_ring(q, n):
        if n == 0:
            thin_own[q] = move(thin_inputs[q], thin.at[q, y, c])
            mine = piece(q, y, None)
            thin_last[q] = [
                put(thin_inputs[q], mine, ts.at[q, 0, 0], tr.at[q, 0, 0], up),
                put(thin_inputs[q], mine, ts.at[q, 1, 0], tr.at[q, 1, 0], down),
            ]
            return
        arrived(thin_last[q])
        below, above = wrap(y - n, NY), wrap(y + n, NY)
        if n < NY // 2:
            last = n == NY // 2 - 1
            low, high = piece(q, below, 0 if last else None), piece(q, above, 1 if last else None)
            thin_last[q] = [
                put(low, low, ts.at[q, 0, n], tr.at[q, 0, n], up),
                put(high, high, ts.at[q, 1, n], tr.at[q, 1, n], down),
            ]
        else:
            thin_own[q].wait()
            mine = thin.at[q, :, c]
            thin_core[q] = [put(mine, mine, tcs.at[q], tcr.at[q], dev(c=1 - c))]

    ag = {}

    def ag_start(i, buf, src):
        mine = buf.at[row]
        ag[i] = [put(src, mine, ah_s.at[i], ah_r.at[i], dev(h=1 - h))]
        for d in range(NX - 1):
            ag[i].append(put(src, mine, ax_s.at[i, 0, d], ax_r.at[i, 0, d], x_peers[d]))

    def ag_forward(i, buf):
        ag[i][0].wait_recv()
        other = buf.at[x * NH + 1 - h]
        for d in range(NX - 1):
            ag[i].append(put(other, other, ax_s.at[i, 1, d], ax_r.at[i, 1, d], x_peers[d]))

    def ag_wait(i):
        arrived(ag[i][1:])

    def times(i, p):
        def one(k, total):
            return total + dot_nn(cols[i, k], panel[p, k].reshape(COLS, COLS))

        return lax.fori_loop(0, NY, one, jnp.zeros((ROWS, COLS), F32))

    class Sum:
        def __init__(self, j, part, part16, got, send_half, got_half):
            self.j, self.part, self.part16, self.got = j, part, part16, got
            self.send_half, self.got_half = send_half, got_half
            self.x_copies = [None, None]

        def start(self, g, term):
            j, part, part16, got = self.j, self.part, self.part16, self.got
            to_h = 1 - h if g == 0 else h

            @pl.loop(0, NX)
            def _(k):
                value = term(k * NH + to_h)
                part[g, k] = value
                part16[g, k] = value.astype(BF16)

            self.x_copies[g] = [
                put(
                    part16.at[g, wrap(x + d + 1, NX)], got.at[g, d],
                    rx_s.at[j, g, d], rx_r.at[j, g, d], x_peers[d],
                )
                for d in range(NX - 1)
            ]

        def total(self, g):
            arrived(self.x_copies[g])
            got = self.got
            return self.part[g, x] + got[g, 0].astype(F32) + got[g, 1].astype(F32) + got[g, 2].astype(F32)

        def middle(self):
            self.send_half[...] = self.total(0).astype(BF16)
            self.h_copy = put(self.send_half, self.got_half, rh_s.at[self.j], rh_r.at[self.j], dev(h=1 - h))

        def end(self):
            total = self.total(1)
            self.h_copy.wait_recv()
            return total + self.got_half[...].astype(F32)

    sums = [
        Sum(j, part.at[j], part16.at[j], got.at[j], send_half.at[j], got_half.at[j]) for j in range(3)
    ]
    sum_d, sum_lt, sum_ld = sums
    sum_mg = Sum(3, part3, part3_16, got3, send_half3, got_half3)

    def inner(left, p):
        return lambda k: dot_nt(left[...], panel[p, k].reshape(COLS, COLS))

    CT, CU, CX = range(3)
    keep = []

    u_swap = []

    def u_send():
        keep.append(move(u_ref.at[:, pl.ds(l * SUB, SUB)], cols3.at[row, pl.ds(l * ROWS, ROWS)]))
        for d in range(NL - 1):
            lane = pl.ds(wrap(l + d + 1, NL) * SUB, SUB)
            u_swap.append(put(u_ref.at[:, lane], cols3.at[row, pl.ds(l * ROWS, ROWS)], us.at[d], ur.at[d], l_peers[d]))

    def u_start():
        keep[-1].wait()
        arrived(u_swap)
        ag_start(3, cols3, cols3.at[row])

    e_copies = []

    def e_partial():
        ag_wait(3)
        arrived(thin_core[TD])

        def one(k, total):
            return total + dot_nn(cols3[k], thin[TD, k].reshape(SUB, COLS))

        value = lax.fori_loop(0, NY, one, jnp.zeros((NL * ROWS, COLS), F32))
        for k in range(NL):
            ez[k] = value[k * ROWS:(k + 1) * ROWS]
            ez16[k] = value[k * ROWS:(k + 1) * ROWS].astype(BF16)
        for d in range(NL - 1):
            e_copies.append(put(ez16.at[wrap(l + d + 1, NL)], got_e.at[d], es.at[d], er.at[d], l_peers[d]))

    def e_total():
        arrived(e_copies)
        return ez[l] + got_e[0].astype(F32) + got_e[1].astype(F32) + got_e[2].astype(F32)

    g_copies, q_copies = [], []

    def g_send():
        keep.append(move(gb, gz.at[l]))
        for d in range(NL - 1):
            g_copies.append(put(gb, gz.at[l], gs.at[d], gr.at[d], l_peers[d]))

    def mg_start(g):
        if g == 0:
            keep[-1].wait()
            arrived(g_copies)
            arrived(thin_core[M])
        sum_mg.start(g, lambda k: dot_nt(gz[...].reshape(NL * ROWS, COLS), thin[M, k].reshape(SUB, COLS)))

    def mg_end():
        value = sum_mg.end()
        for k in range(NL):
            quarter[k] = value[k * ROWS:(k + 1) * ROWS]
        lane = pl.ds(l * SUB, SUB)
        keep.append(move(quarter.at[l], joined.at[:, lane]))
        for d in range(NL - 1):
            q_copies.append(
                put(quarter.at[wrap(l + d + 1, NL)], joined.at[:, lane], qs.at[d], qr.at[d], l_peers[d])
            )

    z_send(T)
    thin_ring(TD, 0)
    thin_ring(M, 0)
    thin_ring(TD, 1)
    thin_ring(M, 1)
    ring(T, 0)
    ag_start(CU, cols.at[CU], u_ref)
    keep_u = move(u_ref, cols.at[CU, row])
    u_send()
    z_send(S)
    thin_ring(TD, 2)
    thin_ring(M, 2)
    ring(T, 1)
    ring(T, 2)
    ag_forward(CU, cols.at[CU])
    ag_start(CT, cols.at[CT], t_ref)
    keep_t = move(t_ref, cols.at[CT, row])
    thin_ring(TD, 3)
    ring(T, 3)
    thin_ring(M, 3)
    ring(T, 4)
    u_start()
    thin_ring(TD, 4)
    thin_ring(M, 4)
    ring(T, 5)
    ring(S, 0)
    ag_forward(CT, cols.at[CT])
    ring(T, 6)
    ag_forward(3, cols3)
    z_send(U)
    ring(T, 7)
    keep_u.wait()
    ag_wait(CU)
    full(T)
    xb[...] = (mb[...].astype(F32) - times(CU, T)).astype(BF16)
    ag_start(CX, cols.at[CX], xb)
    keep_x = move(xb, cols.at[CX, row])
    ring(S, 1)
    ring(S, 2)
    e_partial()
    ring(S, 3)
    ring(S, 4)
    ag_forward(CX, cols.at[CX])
    ring(S, 5)
    ring(U, 0)
    ring(S, 6)
    ring(S, 7)
    keep_x.wait()
    ag_wait(CX)
    full(S)
    g = times(CX, S)
    gb[...] = g.astype(BF16)
    la_out[...] = (-(pattern * g)).astype(BF16)
    sum_lt.start(0, inner(gb, T))
    ring(U, 1)
    g_send()
    sum_lt.start(1, inner(gb, T))
    keep_t.wait()
    ag_wait(CT)
    ring(U, 2)
    o_out[...] = (-times(CT, S)).astype(BF16)
    sum_lt.middle()
    ring(U, 3)
    mg_start(0)
    mg_start(1)
    ring(U, 4)
    lt_out[...] = (sum_lt.end() - e_total()).astype(BF16)
    ring(U, 5)
    sum_mg.middle()
    sum_d.start(0, inner(o_out, T))
    sum_d.start(1, inner(o_out, T))
    ring(U, 6)
    mg_end()
    ring(U, 7)
    full(U)
    sum_ld.start(0, inner(lt_out, U))
    sum_ld.start(1, inner(lt_out, U))
    sum_d.middle()
    sum_ld.middle()
    d_out[...] = (td_ref[...].astype(F32) - sum_d.end()).astype(BF16)
    keep[-1].wait()
    arrived(q_copies)
    base = ld_ref[...].astype(F32) + joined[...]
    ldiag_out[...] = (base - sum_ld.end()).astype(BF16)
    for copy in sent:
        copy.wait_send()


def finish(*refs):
    for src, dst in zip(refs[:5], refs[5:]):
        dst[...] = src[...]


def body(sigma_anc, top_panel, top_dinv, low_upper, low_ancestor, low_dinv, low_rows):
    block, block3 = (ROWS, COLS), (NL * ROWS, SUB)
    dma, vmem = pltpu.SemaphoreType.DMA, pltpu.VMEM
    shapes = [jax.ShapeDtypeStruct(block, BF16)] * 5
    outs = pl.pallas_call(
        kernel,
        out_shape=shapes,
        in_specs=[pl.BlockSpec(memory_space=pltpu.SMEM)] + [pl.BlockSpec(memory_space=pltpu.VMEM)] * 6,
        out_specs=[pl.BlockSpec(memory_space=pltpu.VMEM)] * 5,
        scratch_shapes=[
            vmem((3, NY, NL, NC) + block, BF16),
            vmem((2, NY, NC) + block, BF16),
            vmem((3, NX * NH) + block, BF16),
            vmem((NX * NH,) + block3, BF16),
            vmem(block, BF16),
            vmem(block, BF16),
            vmem(block, BF16),
            vmem((NL,) + block, BF16),
            vmem((NL,) + block, F32),
            vmem((NL,) + block, BF16),
            vmem((NL - 1,) + block, BF16),
            vmem((3, NH, NX) + block, F32),
            vmem((3, NH, NX) + block, BF16),
            vmem((3, NH, NX - 1) + block, BF16),
            vmem((3,) + block, BF16),
            vmem((3,) + block, BF16),
            vmem((NH, NX) + block3, F32),
            vmem((NH, NX) + block3, BF16),
            vmem((NH, NX - 1) + block3, BF16),
            vmem(block3, BF16),
            vmem(block3, BF16),
            vmem((NL, ROWS, SUB), F32),
            vmem(block, F32),
            dma((12,)),
            dma((3, 3)), dma((3, 3)),
            dma((3, 2, 7)), dma((3, 2, 7)),
            dma((3, 9)), dma((3, 9)),
            dma((2, 2, 4)), dma((2, 2, 4)),
            dma((2,)), dma((2,)),
            dma((3,)), dma((3,)),
            dma((4,)), dma((4,)),
            dma((4, 2, 3)), dma((4, 2, 3)),
            dma((3,)), dma((3,)),
            dma((3,)), dma((3,)),
            dma((4, 2, 3)), dma((4, 2, 3)),
            dma((4,)), dma((4,)),
            dma((3,)), dma((3,)),
        ],
        compiler_params=pltpu.CompilerParams(
            collective_id=0, has_side_effects=True, vmem_limit_bytes=56 * 1024 * 1024
        ),
    )(low_rows, top_panel.T, sigma_anc.T, top_dinv.T, low_upper.T, low_ancestor.T, low_dinv.T)
    outs = pl.pallas_call(
        finish,
        out_shape=shapes,
        in_specs=[pl.BlockSpec(memory_space=pltpu.VMEM)] * 5,
        out_specs=[pl.BlockSpec(memory_space=pltpu.VMEM)] * 5,
    )(*outs)
    return tuple(out.T for out in outs)


def solution(mesh):
    return jax.shard_map(
        body,
        mesh=mesh,
        in_specs=(P("row", "col"),) * 6 + (P(),),
        out_specs=(P("row", "col"),) * 5,
        check_vma=False,
    )
```

```python
import jax
import jax.numpy as jnp
from jax import lax
from jax.experimental import pallas as pl
from jax.experimental.pallas import tpu as pltpu
from jax.sharding import PartitionSpec as P

BLOCK = 128
NX, NH, NY, NL, NC = 4, 2, 8, 4, 2
F32, BF16 = jnp.float32, jnp.bfloat16
T, U, S, TD, M = range(5)
ROWS, COLS = 64, 512
SUB = COLS // NL


def dot_nn(left, right):
    return jnp.dot(left, right, preferred_element_type=F32)


def dot_nt(left, right):
    return lax.dot_general(left, right, (((1,), (1,)), ((), ())), preferred_element_type=F32)


def kernel(
    low_rows, t_ref, s_ref, td_ref, u_ref, a_ref, ld_ref,
    o_out, d_out, lt_out, la_out, ldiag_out,
    panel, thin, cols, mb, xb, gb, gz, ez, ez16, got_e,
    part, part16, got, send_half, got_half,
    part3, part3_16, got3, send_half3, got_half3, quarter, joined,
    local_sem, zs, zr, ys, yr, cs, cr, ts, tr, tcs, tcr, ss, sr,
    ax_s, ax_r, es, er, gs, gr, rx_s, rx_r, rh_s, rh_r, qs, qr,
):
    row, col = lax.axis_index("row"), lax.axis_index("col")
    x, h = row // NH, row % NH
    y, l, c = col // (NL * NC), (col // NC) % NL, col % NC

    def dev(x=x, h=h, y=y, l=l, c=c):
        return (x * NH + h, (y * NL + l) * NC + c)

    def wrap(v, n):
        return lax.rem(v + n, n)

    up, down = dev(y=wrap(y + 1, NY)), dev(y=wrap(y - 1, NY))
    l_peers = [dev(l=wrap(l + d, NL)) for d in range(1, NL)]
    x_peers = [dev(x=wrap(x + d, NX)) for d in range(1, NX)]

    barrier = pltpu.get_barrier_semaphore()
    z_peers = [dev(h=wrap(h + n // NL, NH), l=wrap(l + n % NL, NL)) for n in range(1, NH * NL)]
    peers = z_peers + [up, down, dev(c=1 - c)] + x_peers
    for peer in peers:
        pl.semaphore_signal(barrier, inc=1, device_id=peer, device_id_type=pl.DeviceIdType.MESH)

    blocks = row * (COLS // BLOCK) + lax.broadcasted_iota(jnp.int32, (1, COLS), 1) // BLOCK
    pattern = jnp.zeros((1, COLS), F32)
    for j in range(low_rows.shape[0]):
        pattern = jnp.where(blocks == low_rows[j], 1.0, pattern)
    mb[...] = (a_ref[...].astype(F32) * pattern).astype(BF16)

    pl.semaphore_wait(barrier, len(peers))

    sent = []

    def put(src, dst, send, recv, peer):
        copy = pltpu.make_async_remote_copy(
            src_ref=src, dst_ref=dst, send_sem=send, recv_sem=recv,
            device_id=peer, device_id_type=pl.DeviceIdType.MESH,
        )
        copy.start()
        sent.append(copy)
        return copy

    def arrived(copies):
        for copy in copies:
            copy.wait_recv()

    local = []

    def move(src, dst):
        copy = pltpu.make_async_copy(src, dst, local_sem.at[len(local)])
        copy.start()
        local.append(copy)
        return copy

    inputs = {T: t_ref, U: u_ref}
    own, z_copies, y_copies, c_copies = {}, {}, {}, {}

    def z_send(p):
        own[p] = move(inputs[p], panel.at[p, y, l, c])
        z_copies[p] = [
            put(inputs[p], panel.at[p, y, l, c], zs.at[p, d], zr.at[p, d], l_peers[d]) for d in range(NL - 1)
        ]

    def slab(p, where, part):
        if part is None:
            return panel.at[p, where, :, c]
        return panel.at[p, where, pl.ds(part * (NL // 2), NL // 2), c]

    def to_core(p, where, part):
        ref = slab(p, where, part)
        k = len(c_copies.setdefault(p, []))
        c_copies[p].append(put(ref, ref, cs.at[p, k], cr.at[p, k], dev(c=1 - c)))

    def both(p, n, low, high):
        y_copies.setdefault(p, []).append([
            put(low, low, ys.at[p, 0, n], yr.at[p, 0, n], up),
            put(high, high, ys.at[p, 1, n], yr.at[p, 1, n], down),
        ])

    def ring(p, n):
        if n == 0:
            own[p].wait()
            arrived(z_copies[p])
            both(p, 0, slab(p, y, 0), slab(p, y, 1))
            both(p, 1, slab(p, y, 1), slab(p, y, 0))
            to_core(p, y, None)
            return
        arrived(y_copies[p][n - 1])
        step, second = (n + 1) // 2, (n + 1) % 2
        below, above = wrap(y - step, NY), wrap(y + step, NY)
        if n <= 5:
            both(p, n + 1, slab(p, below, second), slab(p, above, 1 - second))
        if n == 7:
            to_core(p, below, 0)
            to_core(p, above, 1)
        elif second:
            to_core(p, below, None)
            to_core(p, above, None)

    def full(p):
        arrived(c_copies[p])

    slot = {T: 0, S: 1, TD: 2, M: 3}
    groups = {T: (0, 1), S: (1, 3)}
    thin_inputs = [t_ref, s_ref, td_ref, mb]
    thin_own = [move(thin_inputs[k], thin.at[k, y, c]) for k in range(4)]
    thin_last, thin_core = {T: [], S: []}, {T: [], S: []}

    def thin_ring(q, n):
        first, count = groups[q]
        i = 0 if q == T else 1

        def piece(where, part):
            height = pl.ds(0, ROWS) if part is None else pl.ds(part * (ROWS // 2), ROWS // 2)
            return thin.at[pl.ds(first, count), where, c, height]

        def both_ways(k, low, high):
            thin_last[q].append([
                put(low, low, ts.at[i, 0, k], tr.at[i, 0, k], up),
                put(high, high, ts.at[i, 1, k], tr.at[i, 1, k], down),
            ])

        def cross(ref):
            k = len(thin_core[q])
            thin_core[q].append(put(ref, ref, tcs.at[i, k], tcr.at[i, k], dev(c=1 - c)))

        if n == 0:
            for k in range(first, first + count):
                thin_own[k].wait()
            both_ways(0, piece(y, 0), piece(y, 1))
            both_ways(1, piece(y, 1), piece(y, 0))
            cross(piece(y, None))
            return
        arrived(thin_last[q][n - 1])
        step, second = (n + 1) // 2, (n + 1) % 2
        below, above = wrap(y - step, NY), wrap(y + step, NY)
        if n <= 5:
            both_ways(n + 1, piece(below, second), piece(above, 1 - second))
        if n == 7:
            cross(piece(below, 0))
            cross(piece(above, 1))
        elif second:
            cross(piece(below, None))
            cross(piece(above, None))

    def thin_full(q):
        copies = thin_core[T if q == T else S]
        arrived(copies)
        copies.clear()

    spread_z, spread_own, spread_to = {}, {}, {}

    def spread(i, src):
        mine = cols.at[i, x, pl.ds(l * ROWS, ROWS), pl.ds(h * SUB, SUB)]
        spread_own[i] = move(src.at[:, pl.ds(l * SUB, SUB)], mine)
        spread_z[i] = [
            put(
                src.at[:, pl.ds(wrap(l + n % NL, NL) * SUB, SUB)], mine,
                ss.at[i, n - 1], sr.at[i, n - 1], z_peers[n - 1],
            )
            for n in range(1, NH * NL)
        ]

    def spread_x(i):
        spread_own[i].wait()
        arrived(spread_z[i])
        mine = cols.at[i, x]
        spread_to[i] = [put(mine, mine, ax_s.at[i, d], ax_r.at[i, d], x_peers[d]) for d in range(NX - 1)]

    n_copies = {}

    def product(j, i, q):
        thin_full(q)

        def one(k, total):
            return total + dot_nn(cols[i, k], thin[slot[q], pl.ds(k * NH, NH)].reshape(NH * SUB, COLS))

        value = lax.fori_loop(0, NX, one, jnp.zeros((NL * ROWS, COLS), F32))
        for k in range(NL):
            ez[j, k] = value[k * ROWS:(k + 1) * ROWS]
            ez16[j, k] = value[k * ROWS:(k + 1) * ROWS].astype(BF16)
        n_copies[j] = [
            put(ez16.at[j, wrap(l + d + 1, NL)], got_e.at[j, d], es.at[j, d], er.at[j, d], l_peers[d])
            for d in range(NL - 1)
        ]

    def product_total(j):
        arrived(n_copies[j])
        return ez[j, l] + got_e[j, 0].astype(F32) + got_e[j, 1].astype(F32) + got_e[j, 2].astype(F32)

    class Sum:
        def __init__(self, j, part, part16, got, send_half, got_half):
            self.j, self.part, self.part16, self.got = j, part, part16, got
            self.send_half, self.got_half = send_half, got_half
            self.x_copies = [None, None]

        def start(self, g, term):
            j, part, part16, got = self.j, self.part, self.part16, self.got
            to_h = 1 - h if g == 0 else h

            @pl.loop(0, NX)
            def _(k):
                value = term(k * NH + to_h)
                part[g, k] = value
                part16[g, k] = value.astype(BF16)

            self.x_copies[g] = [
                put(
                    part16.at[g, wrap(x + d + 1, NX)], got.at[g, d],
                    rx_s.at[j, g, d], rx_r.at[j, g, d], x_peers[d],
                )
                for d in range(NX - 1)
            ]

        def total(self, g):
            arrived(self.x_copies[g])
            got = self.got
            return self.part[g, x] + got[g, 0].astype(F32) + got[g, 1].astype(F32) + got[g, 2].astype(F32)

        def middle(self):
            self.send_half[...] = self.total(0).astype(BF16)
            self.h_copy = put(self.send_half, self.got_half, rh_s.at[self.j], rh_r.at[self.j], dev(h=1 - h))

        def end(self):
            total = self.total(1)
            self.h_copy.wait_recv()
            return total + self.got_half[...].astype(F32)

    sums = [
        Sum(j, part.at[j], part16.at[j], got.at[j], send_half.at[j], got_half.at[j]) for j in range(3)
    ]
    sum_d, sum_lt, sum_ld = sums
    sum_mg = Sum(3, part3, part3_16, got3, send_half3, got_half3)

    def inner(left, p):
        return lambda k: dot_nt(left[...], panel[p, k].reshape(COLS, COLS))

    CT, CU, CX = range(3)
    PZ, PG, PH, PE = range(4)
    keep = []

    g_copies, q_copies = [], []

    def g_send():
        keep.append(move(gb, gz.at[l]))
        for d in range(NL - 1):
            g_copies.append(put(gb, gz.at[l], gs.at[d], gr.at[d], l_peers[d]))

    def mg_start(g):
        if g == 0:
            keep[-1].wait()
            arrived(g_copies)
            thin_full(M)
        sum_mg.start(g, lambda k: dot_nt(gz[...].reshape(NL * ROWS, COLS), thin[slot[M], k].reshape(SUB, COLS)))

    def mg_end():
        value = sum_mg.end()
        for k in range(NL):
            quarter[k] = value[k * ROWS:(k + 1) * ROWS]
        lane = pl.ds(l * SUB, SUB)
        keep.append(move(quarter.at[l], joined.at[:, lane]))
        for d in range(NL - 1):
            q_copies.append(
                put(quarter.at[wrap(l + d + 1, NL)], joined.at[:, lane], qs.at[d], qr.at[d], l_peers[d])
            )

    thin_ring(T, 0)
    spread(CU, u_ref)
    thin_ring(T, 1)
    spread(CT, t_ref)
    thin_ring(T, 2)
    z_send(T)
    thin_ring(T, 3)
    spread_x(CU)
    thin_ring(T, 4)
    thin_ring(T, 5)
    thin_ring(S, 0)
    thin_ring(T, 6)
    thin_ring(T, 7)
    arrived(spread_to[CU])
    product(PZ, CU, T)
    thin_ring(S, 1)
    spread_x(CT)
    thin_ring(S, 2)
    thin_ring(S, 3)
    thin_ring(S, 4)
    xb[...] = (mb[...].astype(F32) - product_total(PZ)).astype(BF16)
    spread(CX, xb)
    thin_ring(S, 5)
    ring(T, 0)
    z_send(U)
    thin_ring(S, 6)
    spread_x(CX)
    thin_ring(S, 7)
    product(PE, CU, TD)
    ring(T, 1)
    ring(T, 2)
    arrived(spread_to[CX])
    product(PG, CX, S)
    ring(T, 3)
    arrived(spread_to[CT])
    product(PH, CT, S)
    ring(T, 4)
    ring(T, 5)
    ring(U, 0)
    g = product_total(PG)
    gb[...] = g.astype(BF16)
    la_out[...] = (-(pattern * g)).astype(BF16)
    g_send()
    ring(T, 6)
    ring(T, 7)
    full(T)
    sum_lt.start(0, inner(gb, T))
    ring(U, 1)
    sum_lt.start(1, inner(gb, T))
    o_out[...] = (-product_total(PH)).astype(BF16)
    ring(U, 2)
    sum_d.start(0, inner(o_out, T))
    ring(U, 3)
    sum_lt.middle()
    mg_start(0)
    mg_start(1)
    ring(U, 4)
    sum_d.start(1, inner(o_out, T))
    ring(U, 5)
    lt_out[...] = (sum_lt.end() - product_total(PE)).astype(BF16)
    sum_mg.middle()
    ring(U, 6)
    sum_d.middle()
    ring(U, 7)
    full(U)
    sum_ld.start(0, inner(lt_out, U))
    sum_ld.start(1, inner(lt_out, U))
    mg_end()
    sum_ld.middle()
    d_out[...] = (td_ref[...].astype(F32) - sum_d.end()).astype(BF16)
    keep[-1].wait()
    arrived(q_copies)
    base = ld_ref[...].astype(F32) + joined[...]
    ldiag_out[...] = (base - sum_ld.end()).astype(BF16)
    for copy in sent:
        copy.wait_send()


def finish(*refs):
    for src, dst in zip(refs[:5], refs[5:]):
        dst[...] = src[...]


def body(sigma_anc, top_panel, top_dinv, low_upper, low_ancestor, low_dinv, low_rows):
    block, block3 = (ROWS, COLS), (NL * ROWS, SUB)
    dma, vmem = pltpu.SemaphoreType.DMA, pltpu.VMEM
    shapes = [jax.ShapeDtypeStruct(block, BF16)] * 5
    outs = pl.pallas_call(
        kernel,
        out_shape=shapes,
        in_specs=[pl.BlockSpec(memory_space=pltpu.SMEM)] + [pl.BlockSpec(memory_space=pltpu.VMEM)] * 6,
        out_specs=[pl.BlockSpec(memory_space=pltpu.VMEM)] * 5,
        scratch_shapes=[
            vmem((2, NY, NL, NC) + block, BF16),
            vmem((4, NY, NC) + block, BF16),
            vmem((3, NX, NL * ROWS, NH * SUB), BF16),
            vmem(block, BF16),
            vmem(block, BF16),
            vmem(block, BF16),
            vmem((NL,) + block, BF16),
            vmem((4, NL) + block, F32),
            vmem((4, NL) + block, BF16),
            vmem((4, NL - 1) + block, BF16),
            vmem((3, NH, NX) + block, F32),
            vmem((3, NH, NX) + block, BF16),
            vmem((3, NH, NX - 1) + block, BF16),
            vmem((3,) + block, BF16),
            vmem((3,) + block, BF16),
            vmem((NH, NX) + block3, F32),
            vmem((NH, NX) + block3, BF16),
            vmem((NH, NX - 1) + block3, BF16),
            vmem(block3, BF16),
            vmem(block3, BF16),
            vmem((NL, ROWS, SUB), F32),
            vmem(block, F32),
            dma((12,)),
            dma((2, 3)), dma((2, 3)),
            dma((2, 2, 7)), dma((2, 2, 7)),
            dma((2, 9)), dma((2, 9)),
            dma((2, 2, 7)), dma((2, 2, 7)),
            dma((2, 9)), dma((2, 9)),
            dma((3, 7)), dma((3, 7)),
            dma((3, 3)), dma((3, 3)),
            dma((4, 3)), dma((4, 3)),
            dma((3,)), dma((3,)),
            dma((4, 2, 3)), dma((4, 2, 3)),
            dma((4,)), dma((4,)),
            dma((3,)), dma((3,)),
        ],
        compiler_params=pltpu.CompilerParams(
            collective_id=0, has_side_effects=True, vmem_limit_bytes=56 * 1024 * 1024
        ),
    )(low_rows, top_panel.T, sigma_anc.T, top_dinv.T, low_upper.T, low_ancestor.T, low_dinv.T)
    outs = pl.pallas_call(
        finish,
        out_shape=shapes,
        in_specs=[pl.BlockSpec(memory_space=pltpu.VMEM)] * 5,
        out_specs=[pl.BlockSpec(memory_space=pltpu.VMEM)] * 5,
    )(*outs)
    return tuple(out.T for out in outs)


def solution(mesh):
    return jax.shard_map(
        body,
        mesh=mesh,
        in_specs=(P("row", "col"),) * 6 + (P(),),
        out_specs=(P("row", "col"),) * 5,
        check_vma=False,
    )
```

```python
import jax
import jax.numpy as jnp
from jax import lax
from jax.experimental import pallas as pl
from jax.experimental.pallas import tpu as pltpu
from jax.sharding import PartitionSpec as P

BLOCK = 128
NX, NH, NY, NL, NC = 4, 2, 8, 4, 2
F32, BF16 = jnp.float32, jnp.bfloat16
T, U, S, TD, M = range(5)
ROWS, COLS = 64, 512
SUB = COLS // NL


def dot_nn(left, right):
    return jnp.dot(left, right, preferred_element_type=F32)


def dot_nt(left, right):
    return lax.dot_general(left, right, (((1,), (1,)), ((), ())), preferred_element_type=F32)


def kernel(
    low_rows, t_ref, s_ref, td_ref, u_ref, a_ref, ld_ref,
    o_out, d_out, lt_out, la_out, ldiag_out,
    panel, thin, cols, mb, xb, gb, gz, ez, ez16, got_e,
    part, part16, got, send_half, got_half,
    part3, part3_16, got3, send_half3, got_half3, quarter, joined,
    local_sem, zs, zr, ys, yr, cs, cr, ts, tr, tcs, tcr, ss, sr,
    ax_s, ax_r, es, er, gs, gr, rx_s, rx_r, rh_s, rh_r, qs, qr,
):
    row, col = lax.axis_index("row"), lax.axis_index("col")
    x, h = row // NH, row % NH
    y, l, c = col // (NL * NC), (col // NC) % NL, col % NC

    def dev(x=x, h=h, y=y, l=l, c=c):
        return (x * NH + h, (y * NL + l) * NC + c)

    def wrap(v, n):
        return lax.rem(v + n, n)

    up, down = dev(y=wrap(y + 1, NY)), dev(y=wrap(y - 1, NY))
    l_peers = [dev(l=wrap(l + d, NL)) for d in range(1, NL)]
    x_peers = [dev(x=wrap(x + d, NX)) for d in range(1, NX)]

    barrier = pltpu.get_barrier_semaphore()
    z_peers = [dev(h=wrap(h + n // NL, NH), l=wrap(l + n % NL, NL)) for n in range(1, NH * NL)]
    peers = z_peers + [up, down, dev(c=1 - c)] + x_peers
    for peer in peers:
        pl.semaphore_signal(barrier, inc=1, device_id=peer, device_id_type=pl.DeviceIdType.MESH)

    blocks = row * (COLS // BLOCK) + lax.broadcasted_iota(jnp.int32, (1, COLS), 1) // BLOCK
    pattern = jnp.zeros((1, COLS), F32)
    for j in range(low_rows.shape[0]):
        pattern = jnp.where(blocks == low_rows[j], 1.0, pattern)
    mb[...] = (a_ref[...].astype(F32) * pattern).astype(BF16)

    pl.semaphore_wait(barrier, len(peers))

    sent = []

    def put(src, dst, send, recv, peer):
        copy = pltpu.make_async_remote_copy(
            src_ref=src, dst_ref=dst, send_sem=send, recv_sem=recv,
            device_id=peer, device_id_type=pl.DeviceIdType.MESH,
        )
        copy.start()
        sent.append(copy)
        return copy

    def arrived(copies):
        for copy in copies:
            copy.wait_recv()

    local = []

    def move(src, dst):
        copy = pltpu.make_async_copy(src, dst, local_sem.at[len(local)])
        copy.start()
        local.append(copy)
        return copy

    inputs = {T: t_ref, U: u_ref}
    own = {p: move(inputs[p], panel.at[p, y, l, c]) for p in (T, U)}
    z_copies, y_copies, c_copies = {}, {T: {}, U: {}}, {T: [], U: []}
    offsets = {T: [1, 2, 3], U: [0, 1, 2, 3]}
    ends = {T: ([(1, None), (2, 0)], [(3, None), (2, 1)]), U: ([(0, None), (1, None)], [(3, None), (2, None)])}

    def z_send(p):
        z_copies[p] = [
            put(inputs[p], panel.at[p, y, l, c], zs.at[p, d], zr.at[p, d], l_peers[d]) for d in range(NL - 1)
        ]

    def block_at(p, where, offset, part):
        there = wrap(l + offset, NL)
        if part is None:
            return panel.at[p, where, there, c]
        return panel.at[p, where, there, c, pl.ds(part * (ROWS // 2), ROWS // 2)]

    def piece_of(p, side, step, j):
        if step == NY // 2:
            return ends[p][side][j]
        return (offsets[p][j], None) if side == 0 else (offsets[p][-1 - j], None)

    def ring_send(p, step, j):
        k = (step - 1) * len(offsets[p]) + j
        low = block_at(p, wrap(y - step + 1, NY), *piece_of(p, 0, step, j))
        high = block_at(p, wrap(y + step - 1, NY), *piece_of(p, 1, step, j))
        y_copies[p][k] = [
            put(low, low, ys.at[p, 0, k], yr.at[p, 0, k], up),
            put(high, high, ys.at[p, 1, k], yr.at[p, 1, k], down),
        ]

    def to_core(ref, p):
        k = len(c_copies[p])
        c_copies[p].append(put(ref, ref, cs.at[p, k], cr.at[p, k], dev(c=1 - c)))

    def ring(p, m):
        per = len(offsets[p])
        if m == 0:
            if p == U:
                own[p].wait()
            arrived(z_copies[p])
            for j in range(per):
                ring_send(p, 1, j)
            for offset in offsets[p]:
                to_core(block_at(p, y, offset, None), p)
            return
        total = 3 * per + 2
        for k in range((total * (m - 1) + 3) // 7, (total * m + 3) // 7):
            arrived(y_copies[p][k])
            step, j = k // per + 1, k % per
            if step < 3 or (step == 3 and j < 2):
                ring_send(p, step + 1, j)
            to_core(block_at(p, wrap(y - step, NY), *piece_of(p, 0, step, j)), p)
            to_core(block_at(p, wrap(y + step, NY), *piece_of(p, 1, step, j)), p)

    def full(p):
        arrived(c_copies[p])

    slot = {S: 0, TD: 1, M: 2}
    thin_own = [move(ref, thin.at[k, y, c]) for k, ref in enumerate([s_ref, td_ref, mb])]
    thin_last, thin_core = {T: [], S: []}, {T: [], S: []}

    def thin_ring(q, n):
        i = 0 if q == T else 1

        def piece(where, part):
            height = pl.ds(0, ROWS) if part is None else pl.ds(part * (ROWS // 2), ROWS // 2)
            return panel.at[T, where, l, c, height] if q == T else thin.at[:, where, c, height]

        def both_ways(k, low, high):
            thin_last[q].append([
                put(low, low, ts.at[i, 0, k], tr.at[i, 0, k], up),
                put(high, high, ts.at[i, 1, k], tr.at[i, 1, k], down),
            ])

        def cross(ref):
            k = len(thin_core[q])
            thin_core[q].append(put(ref, ref, tcs.at[i, k], tcr.at[i, k], dev(c=1 - c)))

        if n == 0:
            for copy in [own[T]] if q == T else thin_own:
                copy.wait()
            both_ways(0, piece(y, 0), piece(y, 1))
            both_ways(1, piece(y, 1), piece(y, 0))
            cross(piece(y, None))
            return
        arrived(thin_last[q][n - 1])
        step, second = (n + 1) // 2, (n + 1) % 2
        below, above = wrap(y - step, NY), wrap(y + step, NY)
        if n <= 5:
            both_ways(n + 1, piece(below, second), piece(above, 1 - second))
        if n == 7:
            cross(piece(below, 0))
            cross(piece(above, 1))
        elif second:
            cross(piece(below, None))
            cross(piece(above, None))

    def thin_full(q):
        copies = thin_core[T if q == T else S]
        arrived(copies)
        copies.clear()

    spread_z, spread_own, spread_to = {}, {}, {}

    def spread(i, src):
        mine = cols.at[i, x, pl.ds(l * ROWS, ROWS), pl.ds(h * SUB, SUB)]
        spread_own[i] = move(src.at[:, pl.ds(l * SUB, SUB)], mine)
        spread_z[i] = [
            put(
                src.at[:, pl.ds(wrap(l + n % NL, NL) * SUB, SUB)], mine,
                ss.at[i, n - 1], sr.at[i, n - 1], z_peers[n - 1],
            )
            for n in range(1, NH * NL)
        ]

    def spread_x(i, g):
        if g == 0:
            spread_own[i].wait()
        arrived(spread_z[i][:NL - 1] if g == 0 else spread_z[i][NL - 1:])
        mine = cols.at[i, x, :, pl.ds((h if g == 0 else 1 - h) * SUB, SUB)]
        spread_to.setdefault(i, []).extend(
            put(mine, mine, ax_s.at[i, g, d], ax_r.at[i, g, d], x_peers[d]) for d in range(NX - 1)
        )

    n_copies = {}

    def product(j, i, q):
        thin_full(q)

        def one(k, total):
            rows = panel[T, pl.ds(k * NH, NH), l] if q == T else thin[slot[q], pl.ds(k * NH, NH)]
            return total + dot_nn(cols[i, k], rows.reshape(NH * SUB, COLS))

        value = lax.fori_loop(0, NX, one, jnp.zeros((NL * ROWS, COLS), F32))
        for k in range(NL):
            ez[j, k] = value[k * ROWS:(k + 1) * ROWS]
            ez16[j, k] = value[k * ROWS:(k + 1) * ROWS].astype(BF16)
        n_copies[j] = [
            put(ez16.at[j, wrap(l + d + 1, NL)], got_e.at[j, d], es.at[j, d], er.at[j, d], l_peers[d])
            for d in range(NL - 1)
        ]

    def product_total(j):
        arrived(n_copies[j])
        return ez[j, l] + got_e[j, 0].astype(F32) + got_e[j, 1].astype(F32) + got_e[j, 2].astype(F32)

    class Sum:
        def __init__(self, j, part, part16, got, send_half, got_half):
            self.j, self.part, self.part16, self.got = j, part, part16, got
            self.send_half, self.got_half = send_half, got_half
            self.x_copies = [None, None]

        def start(self, g, term):
            j, part, part16, got = self.j, self.part, self.part16, self.got
            to_h = 1 - h if g == 0 else h

            @pl.loop(0, NX)
            def _(k):
                value = term(k * NH + to_h)
                part[g, k] = value
                part16[g, k] = value.astype(BF16)

            self.x_copies[g] = [
                put(
                    part16.at[g, wrap(x + d + 1, NX)], got.at[g, d],
                    rx_s.at[j, g, d], rx_r.at[j, g, d], x_peers[d],
                )
                for d in range(NX - 1)
            ]

        def total(self, g):
            arrived(self.x_copies[g])
            got = self.got
            return self.part[g, x] + got[g, 0].astype(F32) + got[g, 1].astype(F32) + got[g, 2].astype(F32)

        def middle(self):
            self.send_half[...] = self.total(0).astype(BF16)
            self.h_copy = put(self.send_half, self.got_half, rh_s.at[self.j], rh_r.at[self.j], dev(h=1 - h))

        def end(self):
            total = self.total(1)
            self.h_copy.wait_recv()
            return total + self.got_half[...].astype(F32)

    sums = [
        Sum(j, part.at[j], part16.at[j], got.at[j], send_half.at[j], got_half.at[j]) for j in range(3)
    ]
    sum_d, sum_lt, sum_ld = sums
    sum_mg = Sum(3, part3, part3_16, got3, send_half3, got_half3)

    def inner(left, p):
        return lambda k: dot_nt(left[...], panel[p, k].reshape(COLS, COLS))

    CT, CU, CX = range(3)
    PZ, PG, PH, PE = range(4)
    keep = []

    g_copies, q_copies = [], []

    def g_send():
        keep.append(move(gb, gz.at[l]))
        for d in range(NL - 1):
            g_copies.append(put(gb, gz.at[l], gs.at[d], gr.at[d], l_peers[d]))

    def mg_start(g):
        if g == 0:
            keep[-1].wait()
            arrived(g_copies)
            thin_full(M)
        sum_mg.start(g, lambda k: dot_nt(gz[...].reshape(NL * ROWS, COLS), thin[slot[M], k].reshape(SUB, COLS)))

    def mg_end():
        value = sum_mg.end()
        for k in range(NL):
            quarter[k] = value[k * ROWS:(k + 1) * ROWS].astype(BF16)
        lane = pl.ds(l * SUB, SUB)
        keep.append(move(quarter.at[l], joined.at[:, lane]))
        for d in range(NL - 1):
            q_copies.append(
                put(quarter.at[wrap(l + d + 1, NL)], joined.at[:, lane], qs.at[d], qr.at[d], l_peers[d])
            )

    thin_ring(T, 0)
    spread(CU, u_ref)
    thin_ring(S, 0)
    thin_ring(T, 1)
    thin_ring(T, 2)
    z_send(T)
    spread(CT, t_ref)
    spread_x(CU, 0)
    thin_ring(T, 3)
    spread_x(CU, 1)
    thin_ring(T, 4)
    thin_ring(S, 1)
    thin_ring(T, 5)
    z_send(U)
    thin_ring(T, 6)
    thin_ring(S, 2)
    thin_ring(S, 3)
    thin_ring(T, 7)
    arrived(spread_to[CU])
    product(PZ, CU, T)
    spread_x(CT, 0)
    spread_x(CT, 1)
    thin_ring(S, 4)
    thin_ring(S, 5)
    ring(T, 0)
    xb[...] = (mb[...].astype(F32) - product_total(PZ)).astype(BF16)
    spread(CX, xb)
    thin_ring(S, 6)
    thin_ring(S, 7)
    ring(T, 1)
    product(PE, CU, TD)
    spread_x(CX, 0)
    ring(T, 2)
    spread_x(CX, 1)
    ring(U, 0)
    arrived(spread_to[CT])
    product(PH, CT, S)
    ring(T, 3)
    ring(T, 4)
    arrived(spread_to[CX])
    product(PG, CX, S)
    ring(T, 5)
    ring(U, 1)
    ring(T, 6)
    ring(T, 7)
    ring(U, 2)
    full(T)
    g = product_total(PG)
    gb[...] = g.astype(BF16)
    sum_lt.start(0, inner(gb, T))
    g_send()
    ring(U, 3)
    sum_lt.start(1, inner(gb, T))
    la_out[...] = (-(pattern * g)).astype(BF16)
    ring(U, 4)
    o_out[...] = (-product_total(PH)).astype(BF16)
    sum_d.start(0, inner(o_out, T))
    sum_lt.middle()
    ring(U, 5)
    mg_start(0)
    mg_start(1)
    ring(U, 6)
    sum_d.middle()
    ring(U, 7)
    lt_out[...] = (sum_lt.end() - product_total(PE)).astype(BF16)
    full(U)
    sum_ld.start(0, inner(lt_out, U))
    sum_mg.middle()
    sum_ld.start(1, inner(lt_out, U))
    sum_d.start(1, inner(o_out, T))
    sum_ld.middle()
    mg_end()
    d_out[...] = (td_ref[...].astype(F32) - sum_d.end()).astype(BF16)
    keep[-1].wait()
    arrived(q_copies)
    base = ld_ref[...].astype(F32) + joined[...].astype(F32)
    ldiag_out[...] = (base - sum_ld.end()).astype(BF16)
    for copy in sent:
        copy.wait_send()


def finish(*refs):
    for src, dst in zip(refs[:5], refs[5:]):
        dst[...] = src[...]


def body(sigma_anc, top_panel, top_dinv, low_upper, low_ancestor, low_dinv, low_rows):
    block, block3 = (ROWS, COLS), (NL * ROWS, SUB)
    dma, vmem = pltpu.SemaphoreType.DMA, pltpu.VMEM
    shapes = [jax.ShapeDtypeStruct(block, BF16)] * 5
    outs = pl.pallas_call(
        kernel,
        out_shape=shapes,
        in_specs=[pl.BlockSpec(memory_space=pltpu.SMEM)] + [pl.BlockSpec(memory_space=pltpu.VMEM)] * 6,
        out_specs=[pl.BlockSpec(memory_space=pltpu.VMEM)] * 5,
        scratch_shapes=[
            vmem((2, NY, NL, NC) + block, BF16),
            vmem((3, NY, NC) + block, BF16),
            vmem((3, NX, NL * ROWS, NH * SUB), BF16),
            vmem(block, BF16),
            vmem(block, BF16),
            vmem(block, BF16),
            vmem((NL,) + block, BF16),
            vmem((4, NL) + block, F32),
            vmem((4, NL) + block, BF16),
            vmem((4, NL - 1) + block, BF16),
            vmem((3, NH, NX) + block, F32),
            vmem((3, NH, NX) + block, BF16),
            vmem((3, NH, NX - 1) + block, BF16),
            vmem((3,) + block, BF16),
            vmem((3,) + block, BF16),
            vmem((NH, NX) + block3, F32),
            vmem((NH, NX) + block3, BF16),
            vmem((NH, NX - 1) + block3, BF16),
            vmem(block3, BF16),
            vmem(block3, BF16),
            vmem((NL, ROWS, SUB), BF16),
            vmem(block, BF16),
            dma((12,)),
            dma((2, 3)), dma((2, 3)),
            dma((2, 2, 14)), dma((2, 2, 14)),
            dma((2, 32)), dma((2, 32)),
            dma((2, 2, 7)), dma((2, 2, 7)),
            dma((2, 9)), dma((2, 9)),
            dma((3, 7)), dma((3, 7)),
            dma((3, 2, 3)), dma((3, 2, 3)),
            dma((4, 3)), dma((4, 3)),
            dma((3,)), dma((3,)),
            dma((4, 2, 3)), dma((4, 2, 3)),
            dma((4,)), dma((4,)),
            dma((3,)), dma((3,)),
        ],
        compiler_params=pltpu.CompilerParams(
            collective_id=0, has_side_effects=True, vmem_limit_bytes=56 * 1024 * 1024
        ),
    )(low_rows, top_panel.T, sigma_anc.T, top_dinv.T, low_upper.T, low_ancestor.T, low_dinv.T)
    outs = pl.pallas_call(
        finish,
        out_shape=shapes,
        in_specs=[pl.BlockSpec(memory_space=pltpu.VMEM)] * 5,
        out_specs=[pl.BlockSpec(memory_space=pltpu.VMEM)] * 5,
    )(*outs)
    return tuple(out.T for out in outs)


def solution(mesh):
    return jax.shard_map(
        body,
        mesh=mesh,
        in_specs=(P("row", "col"),) * 6 + (P(),),
        out_specs=(P("row", "col"),) * 5,
        check_vma=False,
    )
```

```python
import jax
import jax.numpy as jnp
from jax import lax
from jax.experimental import pallas as pl
from jax.experimental.pallas import tpu as pltpu
from jax.sharding import PartitionSpec as P

BLOCK = 128
NX, NH, NY, NL, NC = 4, 2, 8, 4, 2
F32, BF16 = jnp.float32, jnp.bfloat16
T, U, S, TD, M = range(5)
ROWS, COLS = 64, 512
SUB = COLS // NL


def dot_nn(left, right):
    return jnp.dot(left, right, preferred_element_type=F32)


def dot_nt(left, right):
    return lax.dot_general(left, right, (((1,), (1,)), ((), ())), preferred_element_type=F32)


def kernel(
    low_rows, t_in, s_in, td_in, u_in, a_in, ld_in,
    o_out, d_out, lt_out, la_out, ldiag_out,
    loaded, panel, thin, cols, mb, xb, gb, gz, ez, ez16, got_e,
    part, part16, got, send_half, got_half,
    part3, part3_16, got3, send_half3, got_half3, quarter, joined,
    load_sem, local_sem, zs, zr, ys, yr, cs, cr, ts, tr, tcs, tcr, ss, sr,
    ax_s, ax_r, es, er, gs, gr, rx_s, rx_r, rh_s, rh_r, qs, qr,
):
    row, col = lax.axis_index("row"), lax.axis_index("col")
    x, h = row // NH, row % NH
    y, l, c = col // (NL * NC), (col // NC) % NL, col % NC

    def dev(x=x, h=h, y=y, l=l, c=c):
        return (x * NH + h, (y * NL + l) * NC + c)

    def wrap(v, n):
        return lax.rem(v + n, n)

    up, down = dev(y=wrap(y + 1, NY)), dev(y=wrap(y - 1, NY))
    l_peers = [dev(l=wrap(l + d, NL)) for d in range(1, NL)]
    x_peers = [dev(x=wrap(x + d, NX)) for d in range(1, NX)]

    loads = [
        pltpu.make_async_copy(ref, loaded.at[k], load_sem.at[k])
        for k, ref in enumerate([t_in, u_in, s_in, td_in, a_in, ld_in])
    ]
    for load in loads:
        load.start()
    t_ref, u_ref, s_ref, td_ref, a_ref, ld_ref = [loaded.at[k] for k in range(6)]

    barrier = pltpu.get_barrier_semaphore()
    z_peers = [dev(h=wrap(h + n // NL, NH), l=wrap(l + n % NL, NL)) for n in range(1, NH * NL)]
    peers = z_peers + [up, down, dev(c=1 - c)] + x_peers
    for peer in peers:
        pl.semaphore_signal(barrier, inc=1, device_id=peer, device_id_type=pl.DeviceIdType.MESH)

    blocks = row * (COLS // BLOCK) + lax.broadcasted_iota(jnp.int32, (1, COLS), 1) // BLOCK
    pattern = jnp.zeros((1, COLS), F32)
    for j in range(low_rows.shape[0]):
        pattern = jnp.where(blocks == low_rows[j], 1.0, pattern)
    for load in loads:
        load.wait()
    mb[...] = (a_ref[...].astype(F32) * pattern).astype(BF16)

    pl.semaphore_wait(barrier, len(peers))

    sent = []

    def put(src, dst, send, recv, peer):
        copy = pltpu.make_async_remote_copy(
            src_ref=src, dst_ref=dst, send_sem=send, recv_sem=recv,
            device_id=peer, device_id_type=pl.DeviceIdType.MESH,
        )
        copy.start()
        sent.append(copy)
        return copy

    def arrived(copies):
        for copy in copies:
            copy.wait_recv()

    local = []

    def move(src, dst):
        copy = pltpu.make_async_copy(src, dst, local_sem.at[len(local)])
        copy.start()
        local.append(copy)
        return copy

    inputs = {T: t_ref, U: u_ref}
    own = {p: move(inputs[p], panel.at[p, y, l, c]) for p in (T, U)}
    z_copies, y_copies, c_copies = {}, {T: {}, U: {}}, {T: [], U: []}
    offsets = {T: [1, 2, 3], U: [0, 1, 2, 3]}
    ends = {T: ([(1, None), (2, 0)], [(3, None), (2, 1)]), U: ([(0, None), (1, None)], [(3, None), (2, None)])}

    def z_send(p):
        z_copies[p] = [
            put(inputs[p], panel.at[p, y, l, c], zs.at[p, d], zr.at[p, d], l_peers[d]) for d in range(NL - 1)
        ]

    def block_at(p, where, offset, part):
        there = wrap(l + offset, NL)
        if part is None:
            return panel.at[p, where, there, c]
        return panel.at[p, where, there, c, pl.ds(part * (ROWS // 2), ROWS // 2)]

    def piece_of(p, side, step, j):
        if step == NY // 2:
            return ends[p][side][j]
        return (offsets[p][j], None) if side == 0 else (offsets[p][-1 - j], None)

    def ring_send(p, step, j):
        k = (step - 1) * len(offsets[p]) + j
        low = block_at(p, wrap(y - step + 1, NY), *piece_of(p, 0, step, j))
        high = block_at(p, wrap(y + step - 1, NY), *piece_of(p, 1, step, j))
        y_copies[p][k] = [
            put(low, low, ys.at[p, 0, k], yr.at[p, 0, k], up),
            put(high, high, ys.at[p, 1, k], yr.at[p, 1, k], down),
        ]

    def to_core(ref, p):
        k = len(c_copies[p])
        c_copies[p].append(put(ref, ref, cs.at[p, k], cr.at[p, k], dev(c=1 - c)))

    def ring_own(p, first):
        for j in range(first, len(offsets[p])):
            ring_send(p, 1, j)
        for offset in offsets[p]:
            to_core(block_at(p, y, offset, None), p)

    def ring(p, m, first=None):
        per = len(offsets[p])
        if m == 0:
            if p == U:
                own[p].wait()
            arrived(z_copies[p])
            for j in range(per if first is None else first):
                ring_send(p, 1, j)
            if first is None:
                ring_own(p, per)
            return
        total = 3 * per + 2
        for k in range((total * (m - 1) + 3) // 7, (total * m + 3) // 7):
            arrived(y_copies[p][k])
            step, j = k // per + 1, k % per
            if step < 3 or (step == 3 and j < 2):
                ring_send(p, step + 1, j)
            to_core(block_at(p, wrap(y - step, NY), *piece_of(p, 0, step, j)), p)
            to_core(block_at(p, wrap(y + step, NY), *piece_of(p, 1, step, j)), p)

    def full(p):
        arrived(c_copies[p])

    slot = {S: 0, TD: 1, M: 2}
    thin_own = [move(ref, thin.at[k, y, c]) for k, ref in enumerate([s_ref, td_ref, mb])]
    thin_last, thin_core = {T: [], S: []}, {T: [], S: []}

    def thin_ring(q, n):
        i = 0 if q == T else 1

        def piece(where, part):
            height = pl.ds(0, ROWS) if part is None else pl.ds(part * (ROWS // 2), ROWS // 2)
            return panel.at[T, where, l, c, height] if q == T else thin.at[:, where, c, height]

        def both_ways(k, low, high):
            thin_last[q].append([
                put(low, low, ts.at[i, 0, k], tr.at[i, 0, k], up),
                put(high, high, ts.at[i, 1, k], tr.at[i, 1, k], down),
            ])

        def cross(ref):
            k = len(thin_core[q])
            thin_core[q].append(put(ref, ref, tcs.at[i, k], tcr.at[i, k], dev(c=1 - c)))

        if n == 0:
            for copy in [own[T]] if q == T else thin_own:
                copy.wait()
            both_ways(0, piece(y, 0), piece(y, 1))
            both_ways(1, piece(y, 1), piece(y, 0))
            cross(piece(y, None))
            return
        arrived(thin_last[q][n - 1])
        step, second = (n + 1) // 2, (n + 1) % 2
        below, above = wrap(y - step, NY), wrap(y + step, NY)
        if n <= 5:
            both_ways(n + 1, piece(below, second), piece(above, 1 - second))
        if n == 7:
            cross(piece(below, 0))
            cross(piece(above, 1))
        elif second:
            cross(piece(below, None))
            cross(piece(above, None))

    def thin_full(q):
        copies = thin_core[T if q == T else S]
        arrived(copies)
        copies.clear()

    spread_z, spread_own, spread_to = {}, {}, {}

    def spread(i, src):
        mine = cols.at[i, x, pl.ds(l * ROWS, ROWS), pl.ds(h * SUB, SUB)]
        spread_own[i] = move(src.at[:, pl.ds(l * SUB, SUB)], mine)
        spread_z[i] = [
            put(
                src.at[:, pl.ds(wrap(l + n % NL, NL) * SUB, SUB)], mine,
                ss.at[i, n - 1], sr.at[i, n - 1], z_peers[n - 1],
            )
            for n in range(1, NH * NL)
        ]

    def spread_x(i, g):
        if g == 0:
            spread_own[i].wait()
        arrived(spread_z[i][:NL - 1] if g == 0 else spread_z[i][NL - 1:])
        mine = cols.at[i, x, :, pl.ds((h if g == 0 else 1 - h) * SUB, SUB)]
        spread_to.setdefault(i, []).extend(
            put(mine, mine, ax_s.at[i, g, d], ax_r.at[i, g, d], x_peers[d]) for d in range(NX - 1)
        )

    n_copies = {}

    def product(j, i, q):
        thin_full(q)

        def one(k, total):
            rows = panel[T, pl.ds(k * NH, NH), l] if q == T else thin[slot[q], pl.ds(k * NH, NH)]
            return total + dot_nn(cols[i, k], rows.reshape(NH * SUB, COLS))

        value = lax.fori_loop(0, NX, one, jnp.zeros((NL * ROWS, COLS), F32))
        for k in range(NL):
            ez[j, k] = value[k * ROWS:(k + 1) * ROWS]
            ez16[j, k] = value[k * ROWS:(k + 1) * ROWS].astype(BF16)
        n_copies[j] = [
            put(ez16.at[j, wrap(l + d + 1, NL)], got_e.at[j, d], es.at[j, d], er.at[j, d], l_peers[d])
            for d in range(NL - 1)
        ]

    def product_total(j):
        arrived(n_copies[j])
        return ez[j, l] + got_e[j, 0].astype(F32) + got_e[j, 1].astype(F32) + got_e[j, 2].astype(F32)

    class Sum:
        def __init__(self, j, part, part16, got, send_half, got_half):
            self.j, self.part, self.part16, self.got = j, part, part16, got
            self.send_half, self.got_half = send_half, got_half
            self.x_copies = [None, None]

        def start(self, g, term):
            j, part, part16, got = self.j, self.part, self.part16, self.got
            to_h = 1 - h if g == 0 else h

            copies = {}
            for d in (1, 0, 2):
                k = wrap(x + d + 1, NX)
                part16[g, k] = term(k * NH + to_h).astype(BF16)
                copies[d] = put(part16.at[g, k], got.at[g, d], rx_s.at[j, g, d], rx_r.at[j, g, d], x_peers[d])
            part[g] = term(x * NH + to_h)
            self.x_copies[g] = [copies[d] for d in range(NX - 1)]

        def total(self, g):
            arrived(self.x_copies[g])
            got = self.got
            return self.part[g] + got[g, 0].astype(F32) + got[g, 1].astype(F32) + got[g, 2].astype(F32)

        def middle(self):
            self.send_half[...] = self.total(0).astype(BF16)
            self.h_copy = put(self.send_half, self.got_half, rh_s.at[self.j], rh_r.at[self.j], dev(h=1 - h))

        def end(self):
            total = self.total(1)
            self.h_copy.wait_recv()
            return total + self.got_half[...].astype(F32)

    sums = [
        Sum(j, part.at[j], part16.at[j], got.at[j], send_half.at[j], got_half.at[j]) for j in range(3)
    ]
    sum_d, sum_lt, sum_ld = sums
    sum_mg = Sum(3, part3, part3_16, got3, send_half3, got_half3)

    def inner(left, p):
        return lambda k: dot_nt(left[...], panel[p, k].reshape(COLS, COLS))

    CT, CU, CX = range(3)
    PZ, PG, PH, PE = range(4)
    keep = []

    g_copies, q_copies = [], []

    def g_send():
        keep.append(move(gb, gz.at[l]))
        for d in range(NL - 1):
            g_copies.append(put(gb, gz.at[l], gs.at[d], gr.at[d], l_peers[d]))

    def mg_start(g):
        if g == 0:
            keep[-1].wait()
            arrived(g_copies)
            thin_full(M)
        sum_mg.start(g, lambda k: dot_nt(gz[...].reshape(NL * ROWS, COLS), thin[slot[M], k].reshape(SUB, COLS)))

    def mg_end():
        value = sum_mg.end()
        for k in range(NL):
            quarter[k] = value[k * ROWS:(k + 1) * ROWS].astype(BF16)
        lane = pl.ds(l * SUB, SUB)
        keep.append(move(quarter.at[l], joined.at[:, lane]))
        for d in range(NL - 1):
            q_copies.append(
                put(quarter.at[wrap(l + d + 1, NL)], joined.at[:, lane], qs.at[d], qr.at[d], l_peers[d])
            )

    thin_ring(T, 0)
    spread(CU, u_ref)
    thin_ring(S, 0)
    thin_ring(T, 1)
    thin_ring(T, 2)
    z_send(T)
    spread(CT, t_ref)
    spread_x(CU, 0)
    thin_ring(T, 3)
    spread_x(CU, 1)
    thin_ring(T, 4)
    thin_ring(S, 1)
    thin_ring(T, 5)
    z_send(U)
    thin_ring(T, 6)
    thin_ring(S, 2)
    thin_ring(S, 3)
    thin_ring(T, 7)
    arrived(spread_to[CU])
    product(PZ, CU, T)
    spread_x(CT, 0)
    spread_x(CT, 1)
    thin_ring(S, 4)
    thin_ring(S, 5)
    ring(T, 0)
    ring(U, 0, 2)
    xb[...] = (mb[...].astype(F32) - product_total(PZ)).astype(BF16)
    spread(CX, xb)
    thin_ring(S, 6)
    thin_ring(S, 7)
    ring(T, 1)
    product(PE, CU, TD)
    spread_x(CX, 0)
    ring(T, 2)
    spread_x(CX, 1)
    ring_own(U, 2)
    arrived(spread_to[CT])
    product(PH, CT, S)
    ring(T, 3)
    ring(T, 4)
    arrived(spread_to[CX])
    product(PG, CX, S)
    ring(T, 5)
    ring(U, 1)
    ring(T, 6)
    ring(T, 7)
    ring(U, 2)
    full(T)
    g = product_total(PG)
    gb[...] = g.astype(BF16)
    g_send()
    sum_lt.start(0, inner(gb, T))
    ring(U, 3)
    sum_lt.start(1, inner(gb, T))
    ring(U, 4)
    o_out[...] = (-product_total(PH)).astype(BF16)
    sum_d.start(0, inner(o_out, T))
    la_out[...] = (-(pattern * g)).astype(BF16)
    sum_lt.middle()
    ring(U, 5)
    mg_start(0)
    mg_start(1)
    ring(U, 6)
    sum_d.middle()
    ring(U, 7)
    lt_out[...] = (sum_lt.end() - product_total(PE)).astype(BF16)
    sum_mg.middle()
    full(U)
    sum_ld.start(0, inner(lt_out, U))
    sum_ld.start(1, inner(lt_out, U))
    sum_d.start(1, inner(o_out, T))
    mg_end()
    sum_ld.middle()
    d_out[...] = (td_ref[...].astype(F32) - sum_d.end()).astype(BF16)
    keep[-1].wait()
    arrived(q_copies)
    base = ld_ref[...].astype(F32) + joined[...].astype(F32)
    ldiag_out[...] = (base - sum_ld.end()).astype(BF16)
    for copy in sent:
        copy.wait_send()


def finish(*refs):
    for src, dst in zip(refs[:5], refs[5:]):
        dst[...] = src[...]


def body(sigma_anc, top_panel, top_dinv, low_upper, low_ancestor, low_dinv, low_rows):
    block, block3 = (ROWS, COLS), (NL * ROWS, SUB)
    dma, vmem = pltpu.SemaphoreType.DMA, pltpu.VMEM
    shapes = [jax.ShapeDtypeStruct(block, BF16)] * 5
    outs = pl.pallas_call(
        kernel,
        out_shape=shapes,
        in_specs=[pl.BlockSpec(memory_space=pltpu.SMEM)] + [pl.BlockSpec(memory_space=pl.ANY)] * 6,
        out_specs=[pl.BlockSpec(memory_space=pltpu.VMEM)] * 5,
        scratch_shapes=[
            vmem((6,) + block, BF16),
            vmem((2, NY, NL, NC) + block, BF16),
            vmem((3, NY, NC) + block, BF16),
            vmem((3, NX, NL * ROWS, NH * SUB), BF16),
            vmem(block, BF16),
            vmem(block, BF16),
            vmem(block, BF16),
            vmem((NL,) + block, BF16),
            vmem((4, NL) + block, F32),
            vmem((4, NL) + block, BF16),
            vmem((4, NL - 1) + block, BF16),
            vmem((3, NH) + block, F32),
            vmem((3, NH, NX) + block, BF16),
            vmem((3, NH, NX - 1) + block, BF16),
            vmem((3,) + block, BF16),
            vmem((3,) + block, BF16),
            vmem((NH,) + block3, F32),
            vmem((NH, NX) + block3, BF16),
            vmem((NH, NX - 1) + block3, BF16),
            vmem(block3, BF16),
            vmem(block3, BF16),
            vmem((NL, ROWS, SUB), BF16),
            vmem(block, BF16),
            dma((6,)),
            dma((12,)),
            dma((2, 3)), dma((2, 3)),
            dma((2, 2, 14)), dma((2, 2, 14)),
            dma((2, 32)), dma((2, 32)),
            dma((2, 2, 7)), dma((2, 2, 7)),
            dma((2, 9)), dma((2, 9)),
            dma((3, 7)), dma((3, 7)),
            dma((3, 2, 3)), dma((3, 2, 3)),
            dma((4, 3)), dma((4, 3)),
            dma((3,)), dma((3,)),
            dma((4, 2, 3)), dma((4, 2, 3)),
            dma((4,)), dma((4,)),
            dma((3,)), dma((3,)),
        ],
        compiler_params=pltpu.CompilerParams(
            collective_id=0, has_side_effects=True, vmem_limit_bytes=56 * 1024 * 1024
        ),
    )(low_rows, top_panel.T, sigma_anc.T, top_dinv.T, low_upper.T, low_ancestor.T, low_dinv.T)
    outs = pl.pallas_call(
        finish,
        out_shape=shapes,
        in_specs=[pl.BlockSpec(memory_space=pltpu.VMEM)] * 5,
        out_specs=[pl.BlockSpec(memory_space=pltpu.VMEM)] * 5,
    )(*outs)
    return tuple(out.T for out in outs)


def solution(mesh):
    return jax.shard_map(
        body,
        mesh=mesh,
        in_specs=(P("row", "col"),) * 6 + (P(),),
        out_specs=(P("row", "col"),) * 5,
        check_vma=False,
    )
```
